32 devices in a mesh: row: 4 (over x, core), col: 8 (over z, y).
Axes of the slice: x: 2, y: 2, z: 4, core: 2. Of those that a mesh axis runs over, the one named last changes fastest.
Arguments:
- a_window: bfloat16 [8192, 2048], P(('col', 'row')), may hold values from -0.125 to 0.125
- b_tiles: bfloat16 [4096, 4096], P('col', 'row'), may hold values from -6 to 6
- mask_a: int32 [32, 8], P('col'), may hold values from 0 to 1, as said below
- mask_b: int32 [16, 16], P('col', 'row'), may hold values 0 or 1
Outputs:
- product: bfloat16 [8192, 4096], P('col', 'row')
The draws below stay inside these ranges and needn't reach their ends.
Inputs may be any that keep to these rules, and one draw needn't show every extreme that they name: `mask_a`: block flags, 1 for an occupied block; the share of occupied blocks varies from block row to block row.
All inputs are finite; a program needn't handle non-finite values. No bound on the sum of `mask_b` on one device may be relied on, other than what follows from the above.
Results may differ from the reference program's by a relative error of at most 0.001.
Values may be sent and summed in bfloat16 or wider, within the bound.
No kernel may reach another device: no remote copies, remote signals or barrier semaphores. Data moves between devices by JAX's collectives and lax.ppermute only.
A program may use at most 64 MiB of HBM per device.

```python
import jax
import jax.numpy as jnp
from jax import lax

BS = 256
IB = 4
KB = 2
JB = 4
STEPS = 4
GROUPS = 8
ROW_BLOCKS = 32
COL_BLOCKS = 16
N_ROW = 4
N_COL = 8


def draw_mask_a(key, part):
    key_level, key_raw = jax.random.split(jax.random.fold_in(key, 7))
    level = jax.random.randint(key_level, (ROW_BLOCKS, 1), 1, 9)
    raw = jax.random.randint(key_raw, (ROW_BLOCKS, STEPS * KB), 0, 8)
    return (raw < level).astype(jnp.int32)


def with_ends(drawn, key, least, top_value):
    spot = [jax.random.randint(jax.random.fold_in(key, axis), (), 0, length) for axis, length in enumerate(drawn.shape)]
    longest = drawn.shape.index(max(drawn.shape))
    beside = spot[:longest] + [(spot[longest] + 1) % drawn.shape[longest]] + spot[longest + 1:]
    return drawn.at[tuple(spot)].set(least).at[tuple(beside)].set(top_value)


def block_scale(own_key, dims, cuts, smallest, high):
    level, own = 1.0, jax.random.fold_in(own_key, 6)
    for position, blocks in cuts:
        draws = jnp.exp(jax.random.uniform(jax.random.fold_in(own, position), (blocks,), jnp.float32, smallest / len(cuts), high / len(cuts)))
        level = level * jnp.repeat(draws, dims[position] // blocks).reshape([-1 if axis == position else 1 for axis in range(len(dims))])
    return level


def centred(own_key, shape, spread, reach, cuts=(), held_as=jnp.bfloat16):
    array = jax.random.normal(own_key, shape, jnp.float32) * spread
    if len(cuts) > 0:
        array = block_scale(own_key, shape, cuts, -0.22, 0.18) * array
    return jnp.clip(array, min=-reach, max=reach).astype(held_as)


def setup_inputs(seed: int = 0) -> dict:
    seeds = jax.random.split(jax.random.key(seed), 5)
    a_window = centred(seeds[0], (IB * BS * N_COL, STEPS * KB * BS), (STEPS * KB * BS) ** -0.5, 0.125, ((0, 32),))
    b_tiles = centred(seeds[1], (KB * BS * N_COL, JB * BS * N_ROW), 1.0, 6.0, ((0, 8), (1, 4)))
    mask_a = draw_mask_a(jax.random.fold_in(seeds[4], 71), 0)
    mask_b = with_ends((jax.random.randint(seeds[3], (KB * N_COL, COL_BLOCKS), 0, 3) < 2).astype(jnp.int32), jax.random.fold_in(seeds[3], 1), 0, 1)
    return dict(a_window=a_window, b_tiles=b_tiles, mask_a=mask_a, mask_b=mask_b)


def reference(a_window, b_tiles, mask_a, mask_b):
    a_live = (a_window.reshape(ROW_BLOCKS, BS, STEPS * KB, BS) * mask_a[:, None, :, None].astype(jnp.bfloat16)).reshape(ROW_BLOCKS * BS, STEPS * KB * BS)
    b_live = (b_tiles.reshape(KB * GROUPS, BS, COL_BLOCKS, BS) * mask_b[:, None, :, None].astype(jnp.bfloat16)).reshape(KB * GROUPS * BS, COL_BLOCKS * BS)
    a_groups = a_live.reshape(GROUPS, IB * BS, STEPS, KB * BS)
    b_groups = b_live.reshape(GROUPS, KB * BS, COL_BLOCKS * BS)

    def one_group(group):
        a_rows = a_groups[group]
        total = jnp.zeros((IB * BS, COL_BLOCKS * BS), jnp.float32)
        for step in range(STEPS):
            target = ((group + step) % GROUPS).astype(jnp.int32)
            total = total + jnp.dot(a_rows[:, step, :], b_groups[target], preferred_element_type=jnp.float32)
        return total.astype(jnp.bfloat16)

    result = lax.map(one_group, jnp.arange(GROUPS, dtype=jnp.int32))
    return result.reshape(GROUPS * IB * BS, COL_BLOCKS * BS)
```

```python
import functools

import jax
import jax.numpy as jnp
from jax import lax
from jax.experimental import pallas as pl
from jax.experimental.pallas import tpu as pltpu
from jax.sharding import PartitionSpec as P

BS = 256
KB = 2
STEPS = 4

VMEM = pltpu.MemorySpace.VMEM
SMEM = pltpu.MemorySpace.SMEM


def moved(block, axis, target):
    count = lax.axis_size(axis)
    return lax.ppermute(block, axis, [(i, target(i) % count) for i in range(count)])


def mask_tile_kernel(flags, tile, *pieces):
    for column, piece in enumerate(pieces):
        for row in range(tile.shape[0] // BS):
            block = tile[row * BS : (row + 1) * BS, column * BS : (column + 1) * BS]
            live = flags[row, column].astype(jnp.float32).astype(block.dtype)
            piece[row * BS : (row + 1) * BS, :] = block * live


def mask_tile(tile, flags):
    depth, width = tile.shape
    columns = width // BS
    return pl.pallas_call(
        mask_tile_kernel,
        out_shape=[jax.ShapeDtypeStruct((depth, BS), tile.dtype)] * columns,
        in_specs=[pl.BlockSpec(memory_space=SMEM), pl.BlockSpec(memory_space=VMEM)],
        out_specs=[pl.BlockSpec(memory_space=VMEM)] * columns,
        name="mask_tile",
    )(flags, tile)


def mask_rows_kernel(spot, flags, rows, out):
    row = spot[0]
    for column in range(rows.shape[1] // BS):
        block = rows[:, column * BS : (column + 1) * BS]
        live = flags[row, column].astype(jnp.float32).astype(block.dtype)
        out[:, column * BS : (column + 1) * BS] = block * live


def mask_rows(rows, flags, block_row):
    return pl.pallas_call(
        mask_rows_kernel,
        out_shape=jax.ShapeDtypeStruct(rows.shape, rows.dtype),
        in_specs=[
            pl.BlockSpec(memory_space=SMEM),
            pl.BlockSpec(memory_space=SMEM),
            pl.BlockSpec(memory_space=VMEM),
        ],
        out_specs=pl.BlockSpec(memory_space=VMEM),
        name="mask_rows",
    )(block_row[None], flags, rows)


def column_kernel(shards, fresh, spots, *refs):
    lefts = refs[:shards]
    rights = refs[shards : shards + STEPS]
    out = refs[shards + STEPS + (0 if fresh else 1)]
    rows = lefts[0].shape[0]
    for index, left in enumerate(lefts):
        total = None
        for step, right in enumerate(rights):
            depth = right.shape[0]
            term = jnp.dot(
                left[:, step * depth : (step + 1) * depth],
                right[...],
                preferred_element_type=jnp.float32,
            )
            total = term if total is None else total + term
        start = pl.multiple_of(spots[index] * rows, rows)
        out[pl.ds(start, rows), :] = total.astype(out.dtype)


def column_product(spots, lefts, rights, product, column, width):
    shards = len(lefts)
    rows_all = shards * lefts[0].shape[0]
    fresh = product is None
    operands = [spots, *lefts, *rights] + ([] if fresh else [product])
    in_specs = [pl.BlockSpec(memory_space=SMEM)]
    in_specs += [pl.BlockSpec(x.shape, lambda i: (0, 0)) for x in (*lefts, *rights)]
    in_specs += [] if fresh else [pl.BlockSpec(memory_space=pl.ANY)]
    return pl.pallas_call(
        functools.partial(column_kernel, shards, fresh),
        grid=(1,),
        out_shape=jax.ShapeDtypeStruct((rows_all, width), lefts[0].dtype),
        in_specs=in_specs,
        out_specs=pl.BlockSpec((rows_all, BS), lambda i: (0, column)),
        input_output_aliases={} if fresh else {len(operands) - 1: 0},
        cost_estimate=pl.CostEstimate(
            flops=2 * rows_all * lefts[0].shape[1] * BS,
            bytes_accessed=2 * (rows_all * lefts[0].shape[1] + lefts[0].shape[1] * BS + rows_all * BS),
            transcendentals=0,
        ),
        compiler_params=pltpu.CompilerParams(vmem_limit_bytes=24 << 20),
        name="column_product",
    )(*operands)


def shards(a_window, b_tiles, mask_a, mask_b):
    rows = a_window.shape[0]
    n_row = lax.axis_size("row")
    me_row = lax.axis_index("row")
    even = lax.axis_index("col") % 2 == 0

    own = mask_tile(b_tiles, mask_b)
    by_two = [moved(piece, "col", lambda i: i - 2) for piece in own]
    by_one = [
        moved(jnp.where(even, far, near), "col", lambda i: i ^ 1) for far, near in zip(by_two, own)
    ]
    by_three = [moved(piece, "col", lambda i: i - 2) for piece in by_one]

    mine = mask_rows(a_window, mask_a, me_row * rows // BS)
    lefts, spots = [], []
    for distance in range(n_row // 2):
        far = mine if distance == 0 else moved(mine, "row", lambda i: i - 2 * distance)
        lefts += [far, moved(far, "row", lambda i: i ^ 1)]
        place = (me_row + 2 * distance) % n_row
        spots += [place, place ^ 1]
    spots = jnp.stack(spots).astype(jnp.int32)

    product = None
    for column in range(len(own)):
        rights = [own[column], by_one[column], by_two[column], by_three[column]]
        product = column_product(spots, lefts, rights, product, column, b_tiles.shape[1])
    return product


def solution(mesh):
    return jax.shard_map(
        shards,
        mesh=mesh,
        in_specs=(P(("col", "row"), None), P("col", "row"), P("col", None), P("col", "row")),
        out_specs=P("col", "row"),
        check_vma=False,
    )
```

```python
import functools

import jax
import jax.numpy as jnp
from jax import lax
from jax.experimental import pallas as pl
from jax.experimental.pallas import tpu as pltpu
from jax.sharding import PartitionSpec as P

BS = 256
STEPS = 4
PIECES = 4

ANY = pl.ANY
HBM = pltpu.MemorySpace.HBM
VMEM = pltpu.MemorySpace.VMEM


def pinned(value, space=VMEM):
    return pltpu.with_memory_space_constraint(value, space)


def kernel_call(kernel, name, out_shape, operands, spaces, out_space, scratch=(), aliases=None, flops=0):
    moved = 2 * sum(value.size for value in operands)
    return pl.pallas_call(
        kernel,
        out_shape=out_shape,
        in_specs=[pl.BlockSpec(memory_space=space) for space in spaces],
        out_specs=jax.tree.map(lambda _: pl.BlockSpec(memory_space=out_space), out_shape),
        scratch_shapes=list(scratch),
        input_output_aliases=aliases or {},
        cost_estimate=pl.CostEstimate(flops=flops, bytes_accessed=moved, transcendentals=0),
        compiler_params=pltpu.CompilerParams(vmem_limit_bytes=8 << 20),
        name=name,
    )(*operands)


def mask_tile_kernel(first, all_flags, tile, *refs):
    *outs, flags, flag_sem, sem = refs
    width = outs[0].shape[1]
    flag_copy = pltpu.make_async_copy(all_flags, flags, flag_sem)
    flag_copy.start()
    copies = [
        pltpu.make_async_copy(tile.at[:, (first + n) * width : (first + n + 1) * width], out, sem.at[n])
        for n, out in enumerate(outs)
    ]
    for copy in copies:
        copy.start()
    flag_copy.wait()
    for n, (copy, out) in enumerate(zip(copies, outs)):
        copy.wait()
        for row in range(0, out.shape[0], BS):
            for column in range(0, width, BS):

                @pl.when(flags[row // BS, ((first + n) * width + column) // BS] == 0)
                def _():
                    out[row : row + BS, column : column + BS] = jnp.zeros((BS, BS), out.dtype)


def mask_tile(tile, flags, first, count):
    shape = (tile.shape[0], tile.shape[1] // PIECES)
    return kernel_call(
        functools.partial(mask_tile_kernel, first),
        "mask_tile",
        [VMEM(shape, tile.dtype)] * count,
        [pinned(flags, HBM), pinned(tile, HBM)],
        [HBM, HBM],
        VMEM,
        [pltpu.SMEM(flags.shape, flags.dtype), pltpu.SemaphoreType.DMA, pltpu.SemaphoreType.DMA((count,))],
    )


def mask_rows_kernel(all_flags, rows, out, flags, flag_sem, sem):
    flag_copy = pltpu.make_async_copy(all_flags, flags, flag_sem)
    copy = pltpu.make_async_copy(rows, out, sem)
    flag_copy.start()
    copy.start()
    flag_copy.wait()
    copy.wait()
    block_row = lax.axis_index("row") * rows.shape[0] // BS
    for column in range(out.shape[1] // BS):

        @pl.when(flags[block_row, column] == 0)
        def _():
            out[:, column * BS : (column + 1) * BS] = jnp.zeros((out.shape[0], BS), out.dtype)


def mask_rows(rows, flags):
    return kernel_call(
        mask_rows_kernel,
        "mask_rows",
        VMEM(rows.shape, rows.dtype),
        [pinned(flags, HBM), pinned(rows, HBM)],
        [HBM, HBM],
        VMEM,
        [pltpu.SMEM(flags.shape, flags.dtype), pltpu.SemaphoreType.DMA, pltpu.SemaphoreType.DMA],
    )


def choose_kernel(on_even, on_odd, out):
    odd = lax.axis_index("col") % 2

    @pl.when(odd == 0)
    def _():
        out[...] = on_even[...]

    @pl.when(odd == 1)
    def _():
        out[...] = on_odd[...]


def choose(on_even, on_odd):
    return kernel_call(
        choose_kernel,
        "choose",
        VMEM(on_even.shape, on_even.dtype),
        [pinned(on_even), pinned(on_odd)],
        [VMEM, VMEM],
        VMEM,
    )


def stack_rows_kernel(offsets, *refs):
    *shards, out, sem = refs
    rows = shards[0].shape[0]
    me, count = lax.axis_index("row"), len(shards)
    copies = []
    for n, (shard, (distance, flip)) in enumerate(zip(shards, offsets)):
        place = lax.rem(me + distance, count)
        if flip:
            place = place + 1 - 2 * lax.rem(place, 2)
        start = pl.multiple_of(place * rows, rows)
        copies.append(pltpu.make_async_copy(shard, out.at[pl.ds(start, rows), :], sem.at[n]))
    for copy in copies:
        copy.start()
    for copy in copies:
        copy.wait()


def stack_rows(shards, offsets):
    rows, depth = shards[0].shape
    return kernel_call(
        functools.partial(stack_rows_kernel, offsets),
        "stack_rows",
        VMEM((rows * len(shards), depth), shards[0].dtype),
        shards,
        [ANY] * len(shards),
        VMEM,
        [pltpu.SemaphoreType.DMA((len(shards),))],
    )


def product_kernel(plan, left, *refs):
    steps, rights, has_partial, has_product, column = plan
    tiles, rest = refs[:rights], list(refs[rights:])
    partial = rest.pop(0) if has_partial else None
    if has_product:
        rest.pop(0)
    out = rest.pop(0)
    final = len(rest) > 0
    depth, width = tiles[0].shape
    odd = lax.axis_index("col") % 2

    forked = [
        (at, place)
        for at, (_, even, odds) in enumerate(steps)
        for place in range(len(even))
        if even[place] != odds[place]
    ]
    sources = {}
    if forked:
        chosen, fork_sem = rest[2], rest[3]
        for slot, (at, place) in enumerate(forked):
            sources[at, place] = chosen.at[slot]
            for parity in range(2):

                @pl.when(odd == parity)
                def _():
                    source = tiles[steps[at][1 + parity][place]]
                    pltpu.make_async_copy(source, chosen.at[slot], fork_sem.at[slot]).start()

        for slot in range(len(forked)):
            pltpu.make_async_copy(chosen.at[slot], chosen.at[slot], fork_sem.at[slot]).wait()

    places = len(steps[0][1])
    chunk = min(BS, left.shape[0])

    def out_copy(index):
        rows = pl.ds(pl.multiple_of(index * chunk, chunk), chunk)
        return pltpu.make_async_copy(
            rest[0].at[index], out.at[rows, column : column + places * width], rest[1].at[index]
        )

    @pl.loop(0, left.shape[0] // chunk)
    def _(index):
        rows = pl.ds(pl.multiple_of(index * chunk, chunk), chunk)
        for place in range(places):
            columns = slice(place * width, (place + 1) * width)
            total = None
            for at, (step, even, _) in enumerate(steps):
                right = sources.get((at, place), tiles[even[place]])
                term = jnp.dot(
                    left[rows, step * depth : (step + 1) * depth],
                    right[...],
                    preferred_element_type=jnp.float32,
                )
                total = term if total is None else total + term
            if has_partial:
                total = total + partial[rows, columns]
            if final:
                rest[0][index, :, columns] = total.astype(out.dtype)
            else:
                out[rows, columns] = total
        if final:
            out_copy(index).start()

    if final:

        @pl.loop(0, left.shape[0] // chunk)
        def _(index):
            out_copy(index).wait()


def add_products(left, steps, column=0, width=None, partial=None, product=None):
    tiles, numbered, forked = [], [], 0
    for step, *sides in steps:
        entry = [step]
        for pieces in sides:
            for piece in pieces:
                if not any(tile is piece for tile in tiles):
                    tiles.append(piece)
            entry.append(tuple(next(n for n, tile in enumerate(tiles) if tile is piece) for piece in pieces))
        numbered.append(tuple(entry))
        forked += sum(a != b for a, b in zip(entry[1], entry[2]))
    rows, depth, piece_width = left.shape[0], tiles[0].shape[0], tiles[0].shape[1]
    columns = piece_width * len(steps[0][1])
    final = width is not None
    operands = [pinned(x) for x in (left, *tiles, *([] if partial is None else [partial]))]
    spaces = [VMEM] * len(operands)
    aliases = {}
    if product is not None:
        aliases = {len(operands): 0}
        operands.append(product)
        spaces.append(HBM)
    scratch = []
    if final:
        out_shape = jax.ShapeDtypeStruct((rows, width), left.dtype)
        chunk = min(BS, rows)
        scratch += [
            pltpu.VMEM((rows // chunk, chunk, columns), left.dtype),
            pltpu.SemaphoreType.DMA((rows // chunk,)),
        ]
    else:
        out_shape = VMEM((rows, columns), jnp.float32)
    if forked:
        scratch += [pltpu.VMEM((forked, depth, piece_width), left.dtype), pltpu.SemaphoreType.DMA((forked,))]
    plan = (tuple(numbered), len(tiles), partial is not None, product is not None, column)
    return kernel_call(
        functools.partial(product_kernel, plan),
        "add_products",
        out_shape,
        operands,
        spaces,
        HBM if final else VMEM,
        scratch,
        aliases,
        flops=2 * rows * len(steps) * depth * columns,
    )


def moved(block, axis, target):
    count = lax.axis_size(axis)
    return lax.ppermute(block, axis, [(i, target(i) % count) for i in range(count)])


def tied(value, *entries):
    value, *others = lax.optimization_barrier((value, *[entry[0] for entry in entries]))
    for entry, other in zip(entries, others):
        entry[0] = other
    return value


def by_two(block):
    return [moved(block, "col", lambda i: i - 2)]


def across(block):
    return [moved(block, "col", lambda i: i ^ 1)]


def shards(a_window, b_tiles, mask_a, mask_b):
    width = b_tiles.shape[1]
    count = lax.axis_size("row")

    def flip(entry, *held):
        return [moved(tied(entry[0], *held), "row", lambda i: i ^ 1)]

    (own_b,) = mask_tile(b_tiles, mask_b, 0, 1)
    z_b = by_two(own_b)
    d_b = across(own_b)
    own_c, own_1, own_2 = mask_tile(tied(b_tiles, [own_b]), mask_b, 1, 3)
    z_c = by_two(own_c)
    mine = [mask_rows(tied(a_window, [own_c]), mask_a)]

    step = (z_b, d_b)
    s_b = across(tied(z_b[0], *step))
    z_1 = by_two(tied(own_1, *step))
    lefts, offsets, held = [mine], [(0, False)], step
    for distance in range(2, count, 2):
        lefts.append([moved(tied(mine[0], *held), "row", lambda i: i - distance)])
        offsets.append((distance, False))
        held = lefts[-1:]

    step = (z_c, s_b)
    s_c = across(tied(z_c[0], *step))
    z_2 = by_two(tied(own_2, *step))
    near = [flip(mine, *step)]

    step = (z_1, s_c)
    y_1 = across(choose(tied(z_1[0], *step), own_1))
    x_bc = by_two(choose(tied(z_c[0], *step), s_b[0]))

    step = (z_2, y_1)
    y_2 = across(choose(tied(z_2[0], *step), own_2))
    w_1 = by_two(tied(y_1[0], *step))

    step = (x_bc, y_2)
    w_2 = by_two(tied(y_2[0], *step))
    q_c = across(choose(tied(x_bc[0], *step), own_c))
    for left in lefts[1:]:
        near.append(flip(left, *step, *near[-1:]))
    lefts += near
    offsets += [(distance, True) for distance, _ in offsets]
    left = stack_rows([entry[0] for entry in lefts], tuple(offsets))

    partial = add_products(
        left,
        [
            (0, [own_2], [own_2]),
            (1, [y_2[0]], [y_2[0]]),
            (2, [z_2[0]], [z_2[0]]),
        ],
    )
    product = add_products(
        left,
        [
            (0, [own_b, own_c, own_1], [own_b, own_c, own_1]),
            (1, [d_b[0], q_c[0], y_1[0]], [s_b[0], s_c[0], y_1[0]]),
            (2, [z_b[0], z_c[0], z_1[0]], [z_b[0], z_c[0], z_1[0]]),
            (3, [s_b[0], s_c[0], w_1[0]], [x_bc[0], q_c[0], w_1[0]]),
        ],
        width=width,
    )
    return add_products(
        left,
        [(3, [w_2[0]], [w_2[0]])],
        column=3 * (width // PIECES),
        width=width,
        partial=partial,
        product=product,
    )


def solution(mesh):
    return jax.shard_map(
        shards,
        mesh=mesh,
        in_specs=(P(("col", "row"), None), P("col", "row"), P("col", None), P("col", "row")),
        out_specs=P("col", "row"),
        check_vma=False,
    )
```

```python
import functools

import jax
import jax.numpy as jnp
from jax import lax
from jax.experimental import pallas as pl
from jax.experimental.pallas import tpu as pltpu
from jax.sharding import PartitionSpec as P

BS = 256
STEPS = 4
PIECES = 4

ANY = pl.ANY
HBM = pltpu.MemorySpace.HBM
VMEM = pltpu.MemorySpace.VMEM


def pinned(value, space=VMEM):
    return pltpu.with_memory_space_constraint(value, space)


def kernel_call(kernel, name, out_shape, operands, spaces, out_space, scratch=(), aliases=None, flops=0):
    moved = 2 * sum(value.size for value in operands)
    return pl.pallas_call(
        kernel,
        out_shape=out_shape,
        in_specs=[pl.BlockSpec(memory_space=space) for space in spaces],
        out_specs=jax.tree.map(lambda _: pl.BlockSpec(memory_space=out_space), out_shape),
        scratch_shapes=list(scratch),
        input_output_aliases=aliases or {},
        cost_estimate=pl.CostEstimate(flops=flops, bytes_accessed=moved, transcendentals=0),
        compiler_params=pltpu.CompilerParams(vmem_limit_bytes=8 << 20),
        name=name,
    )(*operands)


def mask_tile_kernel(first, all_flags, tile, *refs):
    *outs, flags, flag_sem, sem = refs
    width = outs[0].shape[1]
    flag_copy = pltpu.make_async_copy(all_flags, flags, flag_sem)
    flag_copy.start()
    copies = [
        pltpu.make_async_copy(tile.at[:, (first + n) * width : (first + n + 1) * width], out, sem.at[n])
        for n, out in enumerate(outs)
    ]
    for copy in copies:
        copy.start()
    flag_copy.wait()
    for n, (copy, out) in enumerate(zip(copies, outs)):
        copy.wait()
        for row in range(0, out.shape[0], BS):
            for column in range(0, width, BS):

                @pl.when(flags[row // BS, ((first + n) * width + column) // BS] == 0)
                def _():
                    out[row : row + BS, column : column + BS] = jnp.zeros((BS, BS), out.dtype)


def mask_tile(tile, flags, first, count):
    shape = (tile.shape[0], tile.shape[1] // PIECES)
    return kernel_call(
        functools.partial(mask_tile_kernel, first),
        "mask_tile",
        [VMEM(shape, tile.dtype)] * count,
        [pinned(flags, HBM), pinned(tile, HBM)],
        [HBM, HBM],
        VMEM,
        [pltpu.SMEM(flags.shape, flags.dtype), pltpu.SemaphoreType.DMA, pltpu.SemaphoreType.DMA((count,))],
    )


def mask_rows_kernel(all_flags, rows, out, flags, flag_sem, sem):
    flag_copy = pltpu.make_async_copy(all_flags, flags, flag_sem)
    copy = pltpu.make_async_copy(rows, out, sem)
    flag_copy.start()
    copy.start()
    flag_copy.wait()
    copy.wait()
    block_row = lax.axis_index("row") * rows.shape[0] // BS
    for column in range(out.shape[1] // BS):

        @pl.when(flags[block_row, column] == 0)
        def _():
            out[:, column * BS : (column + 1) * BS] = jnp.zeros((out.shape[0], BS), out.dtype)


def mask_rows(rows, flags):
    return kernel_call(
        mask_rows_kernel,
        "mask_rows",
        VMEM(rows.shape, rows.dtype),
        [pinned(flags, HBM), pinned(rows, HBM)],
        [HBM, HBM],
        VMEM,
        [pltpu.SMEM(flags.shape, flags.dtype), pltpu.SemaphoreType.DMA, pltpu.SemaphoreType.DMA],
    )


def choose_kernel(on_even, on_odd, out):
    odd = lax.axis_index("col") % 2

    @pl.when(odd == 0)
    def _():
        out[...] = on_even[...]

    @pl.when(odd == 1)
    def _():
        out[...] = on_odd[...]


def choose(on_even, on_odd):
    return kernel_call(
        choose_kernel,
        "choose",
        VMEM(on_even.shape, on_even.dtype),
        [pinned(on_even), pinned(on_odd)],
        [VMEM, VMEM],
        VMEM,
    )


def stack_rows_kernel(offsets, *refs):
    *shards, out, sem = refs
    rows = shards[0].shape[0]
    me, count = lax.axis_index("row"), len(shards)
    copies = []
    for n, (shard, (distance, flip)) in enumerate(zip(shards, offsets)):
        place = lax.rem(me + distance, count)
        if flip:
            place = place + 1 - 2 * lax.rem(place, 2)
        start = pl.multiple_of(place * rows, rows)
        copies.append(pltpu.make_async_copy(shard, out.at[pl.ds(start, rows), :], sem.at[n]))
    for copy in copies:
        copy.start()
    for copy in copies:
        copy.wait()


def stack_rows(shards, offsets):
    rows, depth = shards[0].shape
    return kernel_call(
        functools.partial(stack_rows_kernel, offsets),
        "stack_rows",
        VMEM((rows * len(shards), depth), shards[0].dtype),
        shards,
        [ANY] * len(shards),
        VMEM,
        [pltpu.SemaphoreType.DMA((len(shards),))],
    )


def product_kernel(plan, left, *refs):
    places, rights, has_partial, has_product, column = plan
    tiles, rest = refs[:rights], list(refs[rights:])
    partial = rest.pop(0) if has_partial else None
    if has_product:
        rest.pop(0)
    out = rest.pop(0)
    final = len(rest) > 0
    depth, width = tiles[0].shape
    odd = lax.axis_index("col") % 2
    chunk = min(BS, left.shape[0])

    def out_copy(index):
        rows = pl.ds(pl.multiple_of(index * chunk, chunk), chunk)
        columns = slice(column, column + len(places) * width)
        return pltpu.make_async_copy(rest[0].at[index], out.at[rows, columns], rest[1].at[index])

    @pl.loop(0, left.shape[0] // chunk)
    def _(index):
        rows = pl.ds(pl.multiple_of(index * chunk, chunk), chunk)
        for place, terms in enumerate(places):
            columns = slice(place * width, (place + 1) * width)
            total = partial[rows, columns] if has_partial else None
            for number, on_even, on_odd in terms:
                start = on_even * depth
                if on_even != on_odd:
                    start = pl.multiple_of(start + odd * ((on_odd - on_even) * depth), depth)
                term = jnp.dot(
                    left[rows, pl.ds(start, depth)], tiles[number][...], preferred_element_type=jnp.float32
                )
                total = term if total is None else total + term
            if final:
                rest[0][index, :, columns] = total.astype(out.dtype)
            else:
                out[rows, columns] = total
        if final:
            out_copy(index).start()

    if final:

        @pl.loop(0, left.shape[0] // chunk)
        def _(index):
            out_copy(index).wait()


def add_products(left, places, column=0, width=None, partial=None, product=None):
    tiles = []
    for terms in places:
        for tile, _, _ in terms:
            if not any(tile is known for known in tiles):
                tiles.append(tile)
    numbered = tuple(
        tuple((next(n for n, known in enumerate(tiles) if known is tile), a, b) for tile, a, b in terms)
        for terms in places
    )
    rows, piece_width = left.shape[0], tiles[0].shape[1]
    columns = piece_width * len(places)
    final = width is not None
    operands = [pinned(x) for x in (left, *tiles, *([] if partial is None else [partial]))]
    spaces = [VMEM] * len(operands)
    aliases, scratch = {}, []
    if product is not None:
        aliases = {len(operands): 0}
        operands.append(product)
        spaces.append(HBM)
    if final:
        out_shape = jax.ShapeDtypeStruct((rows, width), left.dtype)
        chunk = min(BS, rows)
        scratch += [
            pltpu.VMEM((rows // chunk, chunk, columns), left.dtype),
            pltpu.SemaphoreType.DMA((rows // chunk,)),
        ]
    else:
        out_shape = VMEM((rows, columns), jnp.float32)
    return kernel_call(
        functools.partial(product_kernel, (numbered, len(tiles), partial is not None, product is not None, column)),
        "add_products",
        out_shape,
        operands,
        spaces,
        HBM if final else VMEM,
        scratch,
        aliases,
        flops=2 * rows * tiles[0].shape[0] * piece_width * sum(len(terms) for terms in places),
    )


def moved(block, axis, target):
    count = lax.axis_size(axis)
    return lax.ppermute(block, axis, [(i, target(i) % count) for i in range(count)])


def tied(value, *entries):
    value, *others = lax.optimization_barrier((value, *[entry[0] for entry in entries]))
    for entry, other in zip(entries, others):
        entry[0] = other
    return value


HELD = {
    "Z1": ["Db"],
    "Z2": ["Sb", "Db"],
    "Af": ["Zb", "Db"],
    "Y1": ["Sc", "Zb"],
    "X": ["Zb"],
    "Y2": ["Zb", "Sb"],
    "W1": ["Db", "Zc"],
    "Q": ["X"],
    "Ar": ["X", "Y2", "W1", "Sb", "Zc"],
    "partial2": ["Af"],
    "first": ["W1", "Ar"],
    "last": ["Sb", "Z2", "Db", "Sc"],
    "partial": ["Y1", "X"],
}


def shards(a_window, b_tiles, mask_a, mask_b):
    width = b_tiles.shape[1]
    count = lax.axis_size("row")
    got = {}

    def held(name, value):
        names = HELD.get(name, [])
        return tied(value, *[got[known] for known in names]) if names else value

    def send(name, block, axis, target, key=None):
        with jax.named_scope("send_" + name):
            got[key or name] = [moved(held(name, block), axis, target)]
        return got[key or name][0]

    def by_two(name, block):
        return send(name, block, "col", lambda i: i - 2)

    def across(name, block):
        return send(name, block, "col", lambda i: i ^ 1)

    def value(name):
        return got[name][0]

    (own_b,) = mask_tile(b_tiles, mask_b, 0, 1)
    by_two("Zb", own_b)
    across("Db", own_b)
    own_c, own_1, own_2 = mask_tile(tied(b_tiles, [own_b]), mask_b, 1, 3)
    by_two("Zc", own_c)
    mine = mask_rows(held("rows", tied(a_window, [own_c])), mask_a)

    across("Sb", value("Zb"))
    by_two("Z1", own_1)
    lefts, offsets = [mine], [(0, False)]
    for distance in range(2, count, 2):
        send("Ax", mine, "row", lambda i: i - distance, f"Ax{distance}")
        got["Ax"] = got[f"Ax{distance}"]
        offsets.append((distance, False))
    across("Sc", value("Zc"))
    by_two("Z2", own_2)
    send("Af", mine, "row", lambda i: i ^ 1)
    across("Y1", choose(value("Z1"), own_1))
    by_two("X", choose(value("Zc"), value("Sb")))
    across("Y2", choose(value("Z2"), own_2))
    by_two("W1", value("Y1"))
    by_two("W2", value("Y2"))
    across("Q", choose(value("X"), own_c))
    for distance in range(2, count, 2):
        send("Ar", value(f"Ax{distance}"), "row", lambda i: i ^ 1, f"Ar{distance}")
        got["Ar"] = got[f"Ar{distance}"]
    lefts += [value(f"Ax{distance}") for distance in range(2, count, 2)]
    lefts += [value("Af")] + [value(f"Ar{distance}") for distance in range(2, count, 2)]
    offsets += [(distance, True) for distance, _ in offsets]
    left = stack_rows(lefts, tuple(offsets))
    got["left"] = [left]

    column_b = [(own_b, 0, 0), (value("Zb"), 2, 2), (value("Sb"), 3, 1), (choose(value("Db"), value("X")), 1, 3)]
    column_c = [(own_c, 0, 0), (value("Zc"), 2, 2), (value("Sc"), 3, 1)]
    column_1 = [(own_1, 0, 0), (value("Y1"), 1, 1), (value("Z1"), 2, 2)]
    column_2 = [(own_2, 0, 0), (value("Y2"), 1, 1), (value("Z2"), 2, 2)]
    piece = width // PIECES
    partial = add_products(held("partial", left), [column_c, column_1])
    partial_2 = add_products(held("partial2", left), [column_2])
    product = add_products(held("first", left), [column_b], width=width)
    product = add_products(
        held("middle", left),
        [[(value("Q"), 1, 3)], [(value("W1"), 3, 3)]],
        column=piece,
        width=width,
        partial=partial,
        product=product,
    )
    return add_products(
        held("last", left), [[(value("W2"), 3, 3)]], column=3 * piece, width=width, partial=partial_2, product=product
    )


def solution(mesh):
    return jax.shard_map(
        shards,
        mesh=mesh,
        in_specs=(P(("col", "row"), None), P("col", "row"), P("col", None), P("col", "row")),
        out_specs=P("col", "row"),
        check_vma=False,
    )
```

```python
import functools

import jax
import jax.numpy as jnp
from jax import lax
from jax.experimental import pallas as pl
from jax.experimental.pallas import tpu as pltpu
from jax.sharding import PartitionSpec as P

BS = 256
STEPS = 4
PIECES = 4

ANY = pl.ANY
HBM = pltpu.MemorySpace.HBM
VMEM = pltpu.MemorySpace.VMEM


def pinned(value, space=VMEM):
    return pltpu.with_memory_space_constraint(value, space)


def kernel_call(kernel, name, out_shape, operands, spaces, out_space, scratch=(), flops=0):
    moved = 2 * sum(value.size for value in operands)
    return pl.pallas_call(
        kernel,
        out_shape=out_shape,
        in_specs=[pl.BlockSpec(memory_space=space) for space in spaces],
        out_specs=jax.tree.map(lambda _: pl.BlockSpec(memory_space=out_space), out_shape),
        scratch_shapes=list(scratch),
        cost_estimate=pl.CostEstimate(flops=flops, bytes_accessed=moved, transcendentals=0),
        compiler_params=pltpu.CompilerParams(vmem_limit_bytes=8 << 20),
        name=name,
    )(*operands)


def mask_tile_kernel(first, all_flags, tile, *refs):
    *outs, flags, flag_sem, sem = refs
    width = outs[0].shape[1]
    flag_copy = pltpu.make_async_copy(all_flags, flags, flag_sem)
    flag_copy.start()
    copies = [
        pltpu.make_async_copy(tile.at[:, (first + n) * width : (first + n + 1) * width], out, sem.at[n])
        for n, out in enumerate(outs)
    ]
    for copy in copies:
        copy.start()
    flag_copy.wait()
    for n, (copy, out) in enumerate(zip(copies, outs)):
        copy.wait()
        for row in range(0, out.shape[0], BS):
            for column in range(0, width, BS):

                @pl.when(flags[row // BS, ((first + n) * width + column) // BS] == 0)
                def _():
                    out[row : row + BS, column : column + BS] = jnp.zeros((BS, BS), out.dtype)


def mask_tile(tile, flags, first, count):
    shape = (tile.shape[0], tile.shape[1] // PIECES)
    return kernel_call(
        functools.partial(mask_tile_kernel, first),
        "mask_tile",
        [VMEM(shape, tile.dtype)] * count,
        [pinned(flags, HBM), pinned(tile, HBM)],
        [HBM, HBM],
        VMEM,
        [pltpu.SMEM(flags.shape, flags.dtype), pltpu.SemaphoreType.DMA, pltpu.SemaphoreType.DMA((count,))],
    )


def choose_kernel(on_even, on_odd, out):
    odd = lax.axis_index("col") % 2

    @pl.when(odd == 0)
    def _():
        out[...] = on_even[...]

    @pl.when(odd == 1)
    def _():
        out[...] = on_odd[...]


def choose(on_even, on_odd):
    return kernel_call(
        choose_kernel,
        "choose",
        VMEM(on_even.shape, on_even.dtype),
        [pinned(on_even), pinned(on_odd)],
        [VMEM, VMEM],
        VMEM,
    )


def stack_rows_kernel(offsets, all_flags, *refs):
    *shards, out, flags, flag_sem, sem = refs
    rows = shards[0].shape[0]
    me, count = lax.axis_index("row"), len(shards)
    flag_copy = pltpu.make_async_copy(all_flags, flags, flag_sem)
    flag_copy.start()
    copies = []
    for n, (shard, (distance, flip)) in enumerate(zip(shards, offsets)):
        place = lax.rem(me + distance, count)
        if flip:
            place = place + 1 - 2 * lax.rem(place, 2)
        start = pl.multiple_of(place * rows, rows)
        copies.append(pltpu.make_async_copy(shard, out.at[pl.ds(start, rows), :], sem.at[n]))
    for copy in copies:
        copy.start()
    flag_copy.wait()
    for copy in copies:
        copy.wait()

    @pl.loop(0, out.shape[0] // BS)
    def _(block_row):
        where = pl.ds(pl.multiple_of(block_row * BS, BS), BS)
        for column in range(out.shape[1] // BS):

            @pl.when(flags[block_row, column] == 0)
            def _():
                out[where, column * BS : (column + 1) * BS] = jnp.zeros((BS, BS), out.dtype)


def stack_rows(shards, offsets, flags):
    rows, depth = shards[0].shape
    count = len(shards)
    return kernel_call(
        functools.partial(stack_rows_kernel, offsets),
        "stack_rows",
        VMEM((rows * count, depth), shards[0].dtype),
        [pinned(flags, HBM), *shards],
        [HBM] + [ANY] * count,
        VMEM,
        [pltpu.SMEM(flags.shape, flags.dtype), pltpu.SemaphoreType.DMA, pltpu.SemaphoreType.DMA((count,))],
    )


def sums(left, tiles, places, partial, rows, store):
    depth, width = tiles[0].shape
    odd = lax.axis_index("col") % 2
    for place, terms in enumerate(places):
        columns = slice(place * width, (place + 1) * width)
        total = None if partial is None else partial[rows, columns]
        for number, on_even, on_odd in terms:
            start = on_even * depth
            if on_even != on_odd:
                start = pl.multiple_of(start + odd * ((on_odd - on_even) * depth), depth)
            term = jnp.dot(left[rows, pl.ds(start, depth)], tiles[number][...], preferred_element_type=jnp.float32)
            total = term if total is None else total + term
        store(columns, total)


def chunks_of(left):
    chunk = min(BS, left.shape[0])
    return chunk, left.shape[0] // chunk


def sum_kernel(plan, left, *refs):
    places, rights, has_partial = plan
    partial = refs[rights] if has_partial else None
    out = refs[-1]
    chunk, count = chunks_of(left)

    @pl.loop(0, count)
    def _(index):
        rows = pl.ds(pl.multiple_of(index * chunk, chunk), chunk)

        def store(columns, total):
            out[rows, columns] = total.astype(out.dtype)

        sums(left, refs[:rights], places, partial, rows, store)


def last_kernel(plan, left, *refs):
    places, rights, ready_columns, column = plan
    tiles, partial = refs[:rights], refs[rights]
    ready, (out, result, sem, ready_sem) = refs[rights + 1 : -4], refs[-4:]
    chunk, count = chunks_of(left)
    copies = [
        pltpu.make_async_copy(block, out.at[:, start : start + block.shape[1]], ready_sem.at[n])
        for n, (block, start) in enumerate(zip(ready, ready_columns))
    ]
    for copy in copies:
        copy.start()

    def out_copy(index):
        rows = pl.ds(pl.multiple_of(index * chunk, chunk), chunk)
        return pltpu.make_async_copy(
            result.at[index], out.at[rows, column : column + result.shape[2]], sem.at[index]
        )

    @pl.loop(0, count)
    def _(index):
        rows = pl.ds(pl.multiple_of(index * chunk, chunk), chunk)

        def store(columns, total):
            result[index, :, columns] = total.astype(out.dtype)

        sums(left, tiles, places, partial, rows, store)
        out_copy(index).start()

    for copy in copies:
        copy.wait()

    @pl.loop(0, count)
    def _(index):
        out_copy(index).wait()


def number_terms(places):
    tiles = []
    for terms in places:
        for tile, _, _ in terms:
            if not any(tile is known for known in tiles):
                tiles.append(tile)
    numbered = tuple(
        tuple((next(n for n, known in enumerate(tiles) if known is tile), a, b) for tile, a, b in terms)
        for terms in places
    )
    return tiles, numbered


def add_products(name, left, places, partial=None, dtype=jnp.float32):
    tiles, numbered = number_terms(places)
    rows, width = left.shape[0], tiles[0].shape[1]
    operands = [pinned(x) for x in (left, *tiles, *([] if partial is None else [partial]))]
    return kernel_call(
        functools.partial(sum_kernel, (numbered, len(tiles), partial is not None)),
        "sum_" + name,
        VMEM((rows, width * len(places)), dtype),
        operands,
        [VMEM] * len(operands),
        VMEM,
        flops=2 * rows * tiles[0].size * sum(len(terms) for terms in places),
    )


def finish_product(left, places, column, width, partial, ready):
    tiles, numbered = number_terms(places)
    rows = left.shape[0]
    columns = tiles[0].shape[1] * len(places)
    chunk, count = chunks_of(left)
    operands = [pinned(x) for x in (left, *tiles, partial, *[block for block, _ in ready])]
    plan = (numbered, len(tiles), tuple(start for _, start in ready), column)
    return kernel_call(
        functools.partial(last_kernel, plan),
        "sum_last",
        jax.ShapeDtypeStruct((rows, width), left.dtype),
        operands,
        [VMEM] * len(operands),
        HBM,
        [
            pltpu.VMEM((count, chunk, columns), left.dtype),
            pltpu.SemaphoreType.DMA((count,)),
            pltpu.SemaphoreType.DMA((len(ready),)),
        ],
        flops=2 * rows * tiles[0].size * len(places),
    )


def moved(block, axis, target):
    count = lax.axis_size(axis)
    return lax.ppermute(block, axis, [(i, target(i) % count) for i in range(count)])


def tied(value, *entries):
    value, *others = lax.optimization_barrier((value, *[entry[0] for entry in entries]))
    for entry, other in zip(entries, others):
        entry[0] = other
    return value


HELD = {
    "Ax": ["own_b"],
    "Z1": ["Db", "own_b"],
    "Z2": ["Db", "Zb"],
    "Af": ["Zb", "Z1", "own_c"],
    "Y1": ["own_b", "Sb", "Zb"],
    "X": ["own_c", "own_b", "Sc"],
    "Y2": ["Zb", "Sb", "Y1", "Z2", "Ax", "Z1", "Zc", "Db", "Sc"],
    "W1": ["Y1"],
    "Q": ["Z2", "Db", "X"],
    "Ar": ["X", "Sb", "Zc", "own_b", "Ax", "Sc"],
    "first": ["X", "Sc", "Af", "Z2", "Z1"],
    "last": ["Sc", "Db"],
    "partial": ["X", "Ax", "Db", "own_b", "Z1"],
    "partial2": ["Z1"],
    "middle": ["Y2", "Sb", "Af"],
    "W2": ["Y2", "first", "X"],
    "Sc": ["Sb", "Zc", "own_c"],
    "Sb": ["own_c"],
}


def shards(a_window, b_tiles, mask_a, mask_b):
    width = b_tiles.shape[1]
    count = lax.axis_size("row")
    got = {}

    def held(name, value):
        names = HELD.get(name, [])
        return tied(value, *[got[known] for known in names]) if names else value

    def send(name, block, axis, target, key=None):
        with jax.named_scope("send_" + name):
            got[key or name] = [moved(held(name, block), axis, target)]
        return got[key or name][0]

    def by_two(name, block):
        return send(name, block, "col", lambda i: i - 2)

    def across(name, block):
        return send(name, block, "col", lambda i: i ^ 1)

    def value(name):
        return got[name][0]

    (own_b,) = mask_tile(b_tiles, mask_b, 0, 1)
    got["own_b"] = [own_b]
    by_two("Zb", own_b)
    across("Db", own_b)
    own_c, own_1, own_2 = mask_tile(tied(b_tiles, [own_b]), mask_b, 1, 3)
    got["own_c"] = [own_c]
    by_two("Zc", own_c)
    mine = a_window

    lefts, offsets = [mine], [(0, False)]
    for distance in range(2, count, 2):
        send("Ax", mine, "row", lambda i: i - distance, f"Ax{distance}")
        got["Ax"] = got[f"Ax{distance}"]
        offsets.append((distance, False))
    across("Sb", value("Zb"))
    by_two("Z1", own_1)
    across("Sc", value("Zc"))
    by_two("Z2", own_2)
    send("Af", mine, "row", lambda i: i ^ 1)
    across("Y1", choose(value("Z1"), own_1))
    by_two("X", choose(value("Zc"), value("Sb")))
    across("Y2", choose(value("Z2"), own_2))
    for distance in range(2, count, 2):
        send("Ar", value(f"Ax{distance}"), "row", lambda i: i ^ 1, f"Ar{distance}")
        got["Ar"] = got[f"Ar{distance}"]
    lefts += [value(f"Ax{distance}") for distance in range(2, count, 2)]
    lefts += [value("Af")] + [value(f"Ar{distance}") for distance in range(2, count, 2)]
    offsets += [(distance, True) for distance, _ in offsets]
    left = stack_rows(lefts, tuple(offsets), mask_a)
    by_two("W1", value("Y1"))
    column_c = [(own_c, 0, 0), (value("Zc"), 2, 2), (value("Sc"), 3, 1)]
    column_1 = [(own_1, 0, 0), (value("Y1"), 1, 1), (value("Z1"), 2, 2)]
    got["partial"] = [add_products("partial", held("partial", left), [column_c, column_1])]
    column_2 = [(own_2, 0, 0), (value("Y2"), 1, 1), (value("Z2"), 2, 2)]
    got["partial2"] = [add_products("partial2", held("partial2", left), [column_2])]
    across("Q", choose(value("X"), own_c))
    column_b = [(own_b, 0, 0), (value("Zb"), 2, 2), (value("Sb"), 3, 1), (choose(value("Db"), value("X")), 1, 3)]
    got["first"] = [add_products("first", held("first", left), [column_b], dtype=left.dtype)]
    by_two("W2", value("Y2"))

    piece = width // PIECES
    middle = add_products(
        "middle",
        held("middle", left),
        [[(value("Q"), 1, 3)], [(value("W1"), 3, 3)]],
        partial=value("partial"),
        dtype=left.dtype,
    )
    return finish_product(
        held("last", left),
        [[(value("W2"), 3, 3)]],
        3 * piece,
        width,
        value("partial2"),
        [(value("first"), 0), (middle, piece)],
    )


def solution(mesh):
    return jax.shard_map(
        shards,
        mesh=mesh,
        in_specs=(P(("col", "row"), None), P("col", "row"), P("col", None), P("col", "row")),
        out_specs=P("col", "row"),
        check_vma=False,
    )
```

```python
import functools

import jax
import jax.numpy as jnp
from jax import lax
from jax.experimental import pallas as pl
from jax.experimental.pallas import tpu as pltpu
from jax.sharding import PartitionSpec as P

BS = 256
STEPS = 4
PIECES = 4

ANY = pl.ANY
HBM = pltpu.MemorySpace.HBM
VMEM = pltpu.MemorySpace.VMEM


COST = {
    "choose_b": 12000000000,
    "mask_tile_1": 12000000000,
    "mask_tile_2": 0,
    "sum_last": 3000000000,
    "choose_Y12": 0,
    "choose_X": 1000000000,
    "choose_Q": 6000000000,
    "stack_rows": 12000000000,
    "sum_partial": 6000000000,
    "sum_first": 12000000000,
}


def pinned(value, space=VMEM):
    return pltpu.with_memory_space_constraint(value, space)


def kernel_call(kernel, name, out_shape, operands, spaces, out_space, scratch=(), flops=0):
    moved = 2 * sum(value.size for value in operands)
    return pl.pallas_call(
        kernel,
        out_shape=out_shape,
        in_specs=[pl.BlockSpec(memory_space=space) for space in spaces],
        out_specs=jax.tree.map(lambda _: pl.BlockSpec(memory_space=out_space), out_shape),
        scratch_shapes=list(scratch),
        cost_estimate=pl.CostEstimate(flops=COST.get(name, flops), bytes_accessed=moved, transcendentals=0),
        compiler_params=pltpu.CompilerParams(vmem_limit_bytes=8 << 20),
        name=name,
    )(*operands)


def mask_tile_kernel(spans, all_flags, tile, *refs):
    *outs, flags, flag_sem, sem = refs
    flag_copy = pltpu.make_async_copy(all_flags, flags, flag_sem)
    flag_copy.start()
    copies = [
        pltpu.make_async_copy(tile.at[:, start : start + width], out, sem.at[n])
        for n, ((start, width), out) in enumerate(zip(spans, outs))
    ]
    for copy in copies:
        copy.start()
    flag_copy.wait()
    for (start, width), copy, out in zip(spans, copies, outs):
        copy.wait()
        for row in range(0, out.shape[0], BS):
            for column in range(0, width, BS):

                @pl.when(flags[row // BS, (start + column) // BS] == 0)
                def _():
                    out[row : row + BS, column : column + BS] = jnp.zeros((BS, BS), out.dtype)


def mask_tile(tile, flags, spans):
    count = len(spans)
    return kernel_call(
        functools.partial(mask_tile_kernel, spans),
        "mask_tile_%d" % len(spans),
        [VMEM((tile.shape[0], width), tile.dtype) for _, width in spans],
        [pinned(flags, HBM), pinned(tile, HBM)],
        [HBM, HBM],
        VMEM,
        [pltpu.SMEM(flags.shape, flags.dtype), pltpu.SemaphoreType.DMA, pltpu.SemaphoreType.DMA((count,))],
    )


def choose_kernel(on_even, on_odd, out):
    odd = lax.axis_index("col") % 2

    @pl.when(odd == 0)
    def _():
        out[...] = on_even[...]

    @pl.when(odd == 1)
    def _():
        out[...] = on_odd[...]


def choose(name, on_even, on_odd):
    return kernel_call(
        choose_kernel,
        "choose_" + name,
        VMEM(on_even.shape, on_even.dtype),
        [pinned(on_even), pinned(on_odd)],
        [VMEM, VMEM],
        VMEM,
    )


def stack_rows_kernel(offsets, all_flags, *refs):
    *shards, out, flags, flag_sem, sem = refs
    rows = shards[0].shape[0]
    me, count = lax.axis_index("row"), len(shards)
    flag_copy = pltpu.make_async_copy(all_flags, flags, flag_sem)
    flag_copy.start()
    copies = []
    for n, (shard, (distance, flip)) in enumerate(zip(shards, offsets)):
        place = lax.rem(me + distance, count)
        if flip:
            place = place + 1 - 2 * lax.rem(place, 2)
        start = pl.multiple_of(place * rows, rows)
        copies.append(pltpu.make_async_copy(shard, out.at[pl.ds(start, rows), :], sem.at[n]))
    for copy in copies:
        copy.start()
    flag_copy.wait()
    for copy in copies:
        copy.wait()

    @pl.loop(0, out.shape[0] // BS)
    def _(block_row):
        where = pl.ds(pl.multiple_of(block_row * BS, BS), BS)
        for column in range(out.shape[1] // BS):

            @pl.when(flags[block_row, column] == 0)
            def _():
                out[where, column * BS : (column + 1) * BS] = jnp.zeros((BS, BS), out.dtype)


def stack_rows(shards, offsets, flags):
    rows, depth = shards[0].shape
    count = len(shards)
    return kernel_call(
        functools.partial(stack_rows_kernel, offsets),
        "stack_rows",
        VMEM((rows * count, depth), shards[0].dtype),
        [pinned(flags, HBM), *shards],
        [HBM] + [ANY] * count,
        VMEM,
        [pltpu.SMEM(flags.shape, flags.dtype), pltpu.SemaphoreType.DMA, pltpu.SemaphoreType.DMA((count,))],
    )


def sums(left, tiles, places, partial, rows, store):
    depth = tiles[0].shape[0]
    odd = lax.axis_index("col") % 2
    first = 0
    for terms in places:
        columns = slice(first, first + tiles[terms[0][0]].shape[1])
        first = columns.stop
        total = None if partial is None else partial[rows, columns]
        for number, on_even, on_odd in terms:
            start = on_even * depth
            if on_even != on_odd:
                start = pl.multiple_of(start + odd * ((on_odd - on_even) * depth), depth)
            term = jnp.dot(left[rows, pl.ds(start, depth)], tiles[number][...], preferred_element_type=jnp.float32)
            total = term if total is None else total + term
        store(columns, total)


def chunks_of(left):
    chunk = min(BS, left.shape[0])
    return chunk, left.shape[0] // chunk


def sum_kernel(plan, left, *refs):
    places, rights, has_partial = plan
    partial = refs[rights] if has_partial else None
    out = refs[-1]
    chunk, count = chunks_of(left)

    @pl.loop(0, count)
    def _(index):
        rows = pl.ds(pl.multiple_of(index * chunk, chunk), chunk)

        def store(columns, total):
            out[rows, columns] = total.astype(out.dtype)

        sums(left, refs[:rights], places, partial, rows, store)


def last_kernel(plan, left, *refs):
    places, rights, ready_columns, column = plan
    tiles, partial = refs[:rights], refs[rights]
    ready, (out, result, sem, ready_sem) = refs[rights + 1 : -4], refs[-4:]
    chunk, count = chunks_of(left)
    copies = [
        pltpu.make_async_copy(block, out.at[:, start : start + block.shape[1]], ready_sem.at[n])
        for n, (block, start) in enumerate(zip(ready, ready_columns))
    ]
    for copy in copies:
        copy.start()

    def out_copy(index):
        rows = pl.ds(pl.multiple_of(index * chunk, chunk), chunk)
        return pltpu.make_async_copy(
            result.at[index], out.at[rows, column : column + result.shape[2]], sem.at[index]
        )

    @pl.loop(0, count)
    def _(index):
        rows = pl.ds(pl.multiple_of(index * chunk, chunk), chunk)

        def store(columns, total):
            result[index, :, columns] = total.astype(out.dtype)

        sums(left, tiles, places, partial, rows, store)
        out_copy(index).start()

    for copy in copies:
        copy.wait()

    @pl.loop(0, count)
    def _(index):
        out_copy(index).wait()


def number_terms(places):
    tiles = []
    for terms in places:
        for tile, _, _ in terms:
            if not any(tile is known for known in tiles):
                tiles.append(tile)
    numbered = tuple(
        tuple((next(n for n, known in enumerate(tiles) if known is tile), a, b) for tile, a, b in terms)
        for terms in places
    )
    return tiles, numbered


def add_products(name, left, places, partial=None, dtype=jnp.float32):
    tiles, numbered = number_terms(places)
    rows, columns = left.shape[0], sum(terms[0][0].shape[1] for terms in places)
    operands = [pinned(x) for x in (left, *tiles, *([] if partial is None else [partial]))]
    return kernel_call(
        functools.partial(sum_kernel, (numbered, len(tiles), partial is not None)),
        "sum_" + name,
        VMEM((rows, columns), dtype),
        operands,
        [VMEM] * len(operands),
        VMEM,
        flops=2 * rows * sum(tile.size for terms in places for tile, _, _ in terms),
    )


def finish_product(left, places, column, width, partial, ready):
    tiles, numbered = number_terms(places)
    rows = left.shape[0]
    columns = sum(terms[0][0].shape[1] for terms in places)
    chunk, count = chunks_of(left)
    operands = [pinned(x) for x in (left, *tiles, partial, *[block for block, _ in ready])]
    plan = (numbered, len(tiles), tuple(start for _, start in ready), column)
    return kernel_call(
        functools.partial(last_kernel, plan),
        "sum_last",
        jax.ShapeDtypeStruct((rows, width), left.dtype),
        operands,
        [VMEM] * len(operands),
        HBM,
        [
            pltpu.VMEM((count, chunk, columns), left.dtype),
            pltpu.SemaphoreType.DMA((count,)),
            pltpu.SemaphoreType.DMA((len(ready),)),
        ],
        flops=2 * rows * sum(tile.size for terms in places for tile, _, _ in terms),
    )


def moved(block, axis, target):
    count = lax.axis_size(axis)
    return lax.ppermute(block, axis, [(i, target(i) % count) for i in range(count)])


def tied(value, *entries):
    value, *others = lax.optimization_barrier((value, *[entry[0] for entry in entries]))
    for entry, other in zip(entries, others):
        entry[0] = other
    return value


HELD = {
    "Sb": ["Db", "Zb", "own_c"],
    "Zc": ["Sb"],
    "Q": ["Y12", "Ar", "own_c", "X", "own_b"],
    "Ar": ["Z12", "Zb"],
    "last": ["Zc", "first", "Af", "Db", "Ar", "Zb", "Z12", "Sc", "Q"],
    "first": ["own_c", "X", "Af"],
    "partial": ["Db", "own_b", "Ar", "Sc"],
    "X": ["Z12"],
    "Y12": ["Sb"],
}


def shards(a_window, b_tiles, mask_a, mask_b):
    width = b_tiles.shape[1]
    count = lax.axis_size("row")
    got = {}

    def held(name, value):
        names = HELD.get(name, [])
        return tied(value, *[got[known] for known in names]) if names else value

    def send(name, block, axis, target, key=None):
        with jax.named_scope("send_" + name):
            got[key or name] = [moved(held(name, block), axis, target)]
        return got[key or name][0]

    def by_two(name, block):
        return send(name, block, "col", lambda i: i - 2)

    def across(name, block):
        return send(name, block, "col", lambda i: i ^ 1)

    def value(name):
        return got[name][0]

    piece = width // PIECES
    (own_b,) = mask_tile(b_tiles, mask_b, ((0, piece),))
    got["own_b"] = [own_b]
    by_two("Zb", own_b)
    across("Db", own_b)
    own_c, own_12 = mask_tile(tied(b_tiles, [own_b]), mask_b, ((piece, piece), (2 * piece, 2 * piece)))
    got["own_c"] = [own_c]
    by_two("Z12", own_12)
    mine = a_window

    lefts, offsets = [mine], [(0, False)]
    for distance in range(2, count, 2):
        send("Ax", mine, "row", lambda i: i - distance, f"Ax{distance}")
        got["Ax"] = got[f"Ax{distance}"]
        offsets.append((distance, False))
    across("Sb", value("Zb"))
    send("Af", mine, "row", lambda i: i ^ 1)
    by_two("Zc", own_c)
    across("Y12", choose("Y12", value("Z12"), own_12))
    by_two("X", choose("X", value("Zc"), value("Sb")))
    across("Sc", value("Zc"))
    for distance in range(2, count, 2):
        send("Ar", value(f"Ax{distance}"), "row", lambda i: i ^ 1, f"Ar{distance}")
        got["Ar"] = got[f"Ar{distance}"]
    lefts += [value(f"Ax{distance}") for distance in range(2, count, 2)]
    lefts += [value("Af")] + [value(f"Ar{distance}") for distance in range(2, count, 2)]
    offsets += [(distance, True) for distance, _ in offsets]
    left = stack_rows(lefts, tuple(offsets), mask_a)
    column_b = [(own_b, 0, 0), (value("Zb"), 2, 2), (value("Sb"), 3, 1), (choose("b", value("Db"), value("X")), 1, 3)]
    got["first"] = [add_products("first", held("first", left), [column_b], dtype=left.dtype)]
    by_two("W12", value("Y12"))
    across("Q", choose("Q", value("X"), own_c))

    column_12 = [(own_12, 0, 0), (value("Y12"), 1, 1), (value("Z12"), 2, 2)]
    column_c = [(own_c, 0, 0), (value("Zc"), 2, 2), (value("Sc"), 3, 1)]
    got["partial"] = [add_products("partial", held("partial", left), [column_c, column_12])]
    return finish_product(
        held("last", left),
        [[(value("Q"), 1, 3)], [(value("W12"), 3, 3)]],
        piece,
        width,
        value("partial"),
        [(value("first"), 0)],
    )


def solution(mesh):
    return jax.shard_map(
        shards,
        mesh=mesh,
        in_specs=(P(("col", "row"), None), P("col", "row"), P("col", None), P("col", "row")),
        out_specs=P("col", "row"),
        check_vma=False,
    )
```

```python
import functools

import jax
import jax.numpy as jnp
from jax import lax
from jax.experimental import pallas as pl
from jax.experimental.pallas import tpu as pltpu
from jax.sharding import PartitionSpec as P

BS = 256
STEPS = 4
PIECES = 4

ANY = pl.ANY
HBM = pltpu.MemorySpace.HBM
VMEM = pltpu.MemorySpace.VMEM


COST = {
    "choose_b": 3000000000,
    "mask_tile_1": 0,
    "mask_tile_2": 6000000000,
    "sum_last": 6000000000,
    "choose_Y12": 0,
    "choose_X": 1000000000,
    "choose_Q": 6000000000,
    "stack_rows": 12000000000,
    "sum_early": 3000000000,
}


def pinned(value, space=VMEM):
    return pltpu.with_memory_space_constraint(value, space)


def kernel_call(kernel, name, out_shape, operands, spaces, out_space, scratch=(), flops=0):
    moved = 2 * sum(value.size for value in operands)
    return pl.pallas_call(
        kernel,
        out_shape=out_shape,
        in_specs=[pl.BlockSpec(memory_space=space) for space in spaces],
        out_specs=jax.tree.map(lambda _: pl.BlockSpec(memory_space=out_space), out_shape),
        scratch_shapes=list(scratch),
        cost_estimate=pl.CostEstimate(flops=COST.get(name, flops), bytes_accessed=moved, transcendentals=0),
        compiler_params=pltpu.CompilerParams(vmem_limit_bytes=8 << 20),
        name=name,
    )(*operands)


def mask_tile_kernel(spans, all_flags, tile, *refs):
    *outs, flags, flag_sem, sem = refs
    flag_copy = pltpu.make_async_copy(all_flags, flags, flag_sem)
    flag_copy.start()
    copies = [
        pltpu.make_async_copy(tile.at[:, start : start + width], out, sem.at[n])
        for n, ((start, width), out) in enumerate(zip(spans, outs))
    ]
    for copy in copies:
        copy.start()
    flag_copy.wait()
    for (start, width), copy, out in zip(spans, copies, outs):
        copy.wait()
        for row in range(0, out.shape[0], BS):
            for column in range(0, width, BS):

                @pl.when(flags[row // BS, (start + column) // BS] == 0)
                def _():
                    out[row : row + BS, column : column + BS] = jnp.zeros((BS, BS), out.dtype)


def mask_tile(tile, flags, spans):
    count = len(spans)
    return kernel_call(
        functools.partial(mask_tile_kernel, spans),
        "mask_tile_%d" % len(spans),
        [VMEM((tile.shape[0], width), tile.dtype) for _, width in spans],
        [pinned(flags, HBM), pinned(tile, HBM)],
        [HBM, HBM],
        VMEM,
        [pltpu.SMEM(flags.shape, flags.dtype), pltpu.SemaphoreType.DMA, pltpu.SemaphoreType.DMA((count,))],
    )


def choose_kernel(on_even, on_odd, out):
    odd = lax.axis_index("col") % 2

    @pl.when(odd == 0)
    def _():
        out[...] = on_even[...]

    @pl.when(odd == 1)
    def _():
        out[...] = on_odd[...]


def choose(name, on_even, on_odd):
    return kernel_call(
        choose_kernel,
        "choose_" + name,
        VMEM(on_even.shape, on_even.dtype),
        [pinned(on_even), pinned(on_odd)],
        [VMEM, VMEM],
        VMEM,
    )


def stack_rows_kernel(offsets, all_flags, *refs):
    *shards, out, flags, flag_sem, sem = refs
    rows = shards[0].shape[0]
    me, count = lax.axis_index("row"), len(shards)
    flag_copy = pltpu.make_async_copy(all_flags, flags, flag_sem)
    flag_copy.start()
    copies = []
    for n, (shard, (distance, flip)) in enumerate(zip(shards, offsets)):
        place = lax.rem(me + distance, count)
        if flip:
            place = place + 1 - 2 * lax.rem(place, 2)
        start = pl.multiple_of(place * rows, rows)
        copies.append(pltpu.make_async_copy(shard, out.at[pl.ds(start, rows), :], sem.at[n]))
    for copy in copies:
        copy.start()
    flag_copy.wait()
    for copy in copies:
        copy.wait()

    @pl.loop(0, out.shape[0] // BS)
    def _(block_row):
        where = pl.ds(pl.multiple_of(block_row * BS, BS), BS)
        for column in range(out.shape[1] // BS):

            @pl.when(flags[block_row, column] == 0)
            def _():
                out[where, column * BS : (column + 1) * BS] = jnp.zeros((BS, BS), out.dtype)


def stack_rows(shards, offsets, flags):
    rows, depth = shards[0].shape
    count = len(shards)
    return kernel_call(
        functools.partial(stack_rows_kernel, offsets),
        "stack_rows",
        VMEM((rows * count, depth), shards[0].dtype),
        [pinned(flags, HBM), *shards],
        [HBM] + [ANY] * count,
        VMEM,
        [pltpu.SMEM(flags.shape, flags.dtype), pltpu.SemaphoreType.DMA, pltpu.SemaphoreType.DMA((count,))],
    )


def sums(left, tiles, places, partial, rows, store):
    depth = tiles[0].shape[0]
    odd = lax.axis_index("col") % 2
    first = 0
    for terms in places:
        columns = slice(first, first + tiles[terms[0][0]].shape[1])
        first = columns.stop
        total = None if partial is None else partial[rows, columns]
        for number, on_even, on_odd in terms:
            start = on_even * depth
            if on_even != on_odd:
                start = pl.multiple_of(start + odd * ((on_odd - on_even) * depth), depth)
            term = jnp.dot(left[rows, pl.ds(start, depth)], tiles[number][...], preferred_element_type=jnp.float32)
            total = term if total is None else total + term
        store(columns, total)


def chunks_of(left):
    chunk = min(BS, left.shape[0])
    return chunk, left.shape[0] // chunk


def sum_kernel(plan, left, *refs):
    groups, rights = plan
    tiles, outs = refs[:rights], refs[rights:]
    chunk, count = chunks_of(left)

    @pl.loop(0, count)
    def _(index):
        rows = pl.ds(pl.multiple_of(index * chunk, chunk), chunk)
        for places, out in zip(groups, outs):

            def store(columns, total):
                out[rows, columns] = total.astype(out.dtype)

            sums(left, tiles, places, None, rows, store)


def last_kernel(plan, left, *refs):
    places, rights, ready_columns, column = plan
    tiles, partial = refs[:rights], refs[rights]
    ready, (out, result, sem, ready_sem) = refs[rights + 1 : -4], refs[-4:]
    chunk, count = chunks_of(left)
    copies = [
        pltpu.make_async_copy(block, out.at[:, start : start + block.shape[1]], ready_sem.at[n])
        for n, (block, start) in enumerate(zip(ready, ready_columns))
    ]
    for copy in copies:
        copy.start()

    def out_copy(index):
        rows = pl.ds(pl.multiple_of(index * chunk, chunk), chunk)
        return pltpu.make_async_copy(
            result.at[index], out.at[rows, column : column + result.shape[2]], sem.at[index]
        )

    @pl.loop(0, count)
    def _(index):
        rows = pl.ds(pl.multiple_of(index * chunk, chunk), chunk)

        def store(columns, total):
            result[index, :, columns] = total.astype(out.dtype)

        sums(left, tiles, places, partial, rows, store)
        out_copy(index).start()

    for copy in copies:
        copy.wait()

    @pl.loop(0, count)
    def _(index):
        out_copy(index).wait()


def number_terms(places):
    tiles = []
    for terms in places:
        for tile, _, _ in terms:
            if not any(tile is known for known in tiles):
                tiles.append(tile)
    numbered = tuple(
        tuple((next(n for n, known in enumerate(tiles) if known is tile), a, b) for tile, a, b in terms)
        for terms in places
    )
    return tiles, numbered


def add_products(name, left, groups, dtypes):
    tiles, numbered = number_terms([terms for places in groups for terms in places])
    rows = left.shape[0]
    numbered_groups, out_shapes = [], []
    for places, dtype in zip(groups, dtypes):
        numbered_groups.append(numbered[: len(places)])
        numbered = numbered[len(places) :]
        out_shapes.append(VMEM((rows, sum(terms[0][0].shape[1] for terms in places)), dtype))
    operands = [pinned(x) for x in (left, *tiles)]
    return kernel_call(
        functools.partial(sum_kernel, (tuple(numbered_groups), len(tiles))),
        "sum_" + name,
        out_shapes,
        operands,
        [VMEM] * len(operands),
        VMEM,
        flops=2 * rows * sum(tile.size for places in groups for terms in places for tile, _, _ in terms),
    )


def finish_product(left, places, column, width, partial, ready):
    tiles, numbered = number_terms(places)
    rows = left.shape[0]
    columns = sum(terms[0][0].shape[1] for terms in places)
    chunk, count = chunks_of(left)
    operands = [pinned(x) for x in (left, *tiles, partial, *[block for block, _ in ready])]
    plan = (numbered, len(tiles), tuple(start for _, start in ready), column)
    return kernel_call(
        functools.partial(last_kernel, plan),
        "sum_last",
        jax.ShapeDtypeStruct((rows, width), left.dtype),
        operands,
        [VMEM] * len(operands),
        HBM,
        [
            pltpu.VMEM((count, chunk, columns), left.dtype),
            pltpu.SemaphoreType.DMA((count,)),
            pltpu.SemaphoreType.DMA((len(ready),)),
        ],
        flops=2 * rows * sum(tile.size for terms in places for tile, _, _ in terms),
    )


def moved(block, axis, target):
    count = lax.axis_size(axis)
    return lax.ppermute(block, axis, [(i, target(i) % count) for i in range(count)])


def tied(value, *entries):
    value, *others = lax.optimization_barrier((value, *[entry[0] for entry in entries]))
    for entry, other in zip(entries, others):
        entry[0] = other
    return value


HELD = {
    "Sb": ["Db", "own_c"],
    "Zc": ["Sb"],
    "Q": ["Y12", "Ar", "own_c", "X", "own_b", "Ax"],
    "Ar": ["Z12", "Zb"],
    "last": ["Zc", "Af", "Db", "Ar", "Zb", "Z12", "Sc", "Q"],
    "Y12": ["Sb"],
    "early": ["Af"],
    "W12": ["Z12"],
}


def shards(a_window, b_tiles, mask_a, mask_b):
    width = b_tiles.shape[1]
    count = lax.axis_size("row")
    got = {}

    def held(name, value):
        names = HELD.get(name, [])
        return tied(value, *[got[known] for known in names]) if names else value

    def send(name, block, axis, target, key=None):
        with jax.named_scope("send_" + name):
            got[key or name] = [moved(held(name, block), axis, target)]
        return got[key or name][0]

    def by_two(name, block):
        return send(name, block, "col", lambda i: i - 2)

    def across(name, block):
        return send(name, block, "col", lambda i: i ^ 1)

    def value(name):
        return got[name][0]

    piece = width // PIECES
    (own_b,) = mask_tile(b_tiles, mask_b, ((0, piece),))
    got["own_b"] = [own_b]
    by_two("Zb", own_b)
    across("Db", own_b)
    own_c, own_12 = mask_tile(tied(b_tiles, [own_b]), mask_b, ((piece, piece), (2 * piece, 2 * piece)))
    got["own_c"] = [own_c]
    by_two("Z12", own_12)
    mine = a_window

    lefts, offsets = [mine], [(0, False)]
    for distance in range(2, count, 2):
        send("Ax", mine, "row", lambda i: i - distance, f"Ax{distance}")
        got["Ax"] = got[f"Ax{distance}"]
        offsets.append((distance, False))
    across("Sb", value("Zb"))
    send("Af", mine, "row", lambda i: i ^ 1)
    by_two("Zc", own_c)
    across("Y12", choose("Y12", value("Z12"), own_12))
    by_two("X", choose("X", value("Zc"), value("Sb")))
    across("Sc", value("Zc"))
    for distance in range(2, count, 2):
        send("Ar", value(f"Ax{distance}"), "row", lambda i: i ^ 1, f"Ar{distance}")
        got["Ar"] = got[f"Ar{distance}"]
    lefts += [value(f"Ax{distance}") for distance in range(2, count, 2)]
    lefts += [value("Af")] + [value(f"Ar{distance}") for distance in range(2, count, 2)]
    offsets += [(distance, True) for distance, _ in offsets]
    left = stack_rows(lefts, tuple(offsets), mask_a)
    column_b = [(own_b, 0, 0), (value("Zb"), 2, 2), (value("Sb"), 3, 1), (choose("b", value("Db"), value("X")), 1, 3)]
    by_two("W12", value("Y12"))
    across("Q", choose("Q", value("X"), own_c))

    column_12 = [(own_12, 0, 0), (value("Y12"), 1, 1), (value("Z12"), 2, 2)]
    column_c = [(own_c, 0, 0), (value("Zc"), 2, 2), (value("Sc"), 3, 1)]
    first, partial = add_products(
        "early", held("early", left), [[column_b], [column_c, column_12]], [left.dtype, jnp.float32]
    )
    return finish_product(
        held("last", left),
        [[(value("Q"), 1, 3)], [(value("W12"), 3, 3)]],
        piece,
        width,
        partial,
        [(first, 0)],
    )


def solution(mesh):
    return jax.shard_map(
        shards,
        mesh=mesh,
        in_specs=(P(("col", "row"), None), P("col", "row"), P("col", None), P("col", "row")),
        out_specs=P("col", "row"),
        check_vma=False,
    )
```

```python
import functools

import jax
import jax.numpy as jnp
from jax import lax
from jax.experimental import pallas as pl
from jax.experimental.pallas import tpu as pltpu
from jax.sharding import PartitionSpec as P

BS = 256
STEPS = 4
PIECES = 4

ANY = pl.ANY
HBM = pltpu.MemorySpace.HBM
VMEM = pltpu.MemorySpace.VMEM


COST = {
    "choose_b": 3000000000,
    "mask_tile_1": 0,
    "mask_tile_2": 6000000000,
    "sum_last": 6000000000,
    "choose_Y12": 0,
    "choose_X": 1000000000,
    "choose_Q": 6000000000,
    "stack_rows": 12000000000,
    "sum_early": 3000000000,
}


def pinned(value, space=VMEM):
    return pltpu.with_memory_space_constraint(value, space)


def kernel_call(kernel, name, out_shape, operands, spaces, out_space, scratch=(), flops=0):
    moved = 2 * sum(value.size for value in operands)
    return pl.pallas_call(
        kernel,
        out_shape=out_shape,
        in_specs=[pl.BlockSpec(memory_space=space) for space in spaces],
        out_specs=jax.tree.map(lambda _: pl.BlockSpec(memory_space=out_space), out_shape),
        scratch_shapes=list(scratch),
        cost_estimate=pl.CostEstimate(flops=COST.get(name, flops), bytes_accessed=moved, transcendentals=0),
        compiler_params=pltpu.CompilerParams(vmem_limit_bytes=8 << 20),
        name=name,
    )(*operands)


def mask_tile_kernel(spans, all_flags, tile, *refs):
    *outs, flags, flag_sem, sem = refs
    flag_copy = pltpu.make_async_copy(all_flags, flags, flag_sem)
    flag_copy.start()
    copies = [
        pltpu.make_async_copy(tile.at[:, start : start + width], out, sem.at[n])
        for n, ((start, width), out) in enumerate(zip(spans, outs))
    ]
    for copy in copies:
        copy.start()
    flag_copy.wait()
    for (start, width), copy, out in zip(spans, copies, outs):
        copy.wait()
        for row in range(0, out.shape[0], BS):
            for column in range(0, width, BS):

                @pl.when(flags[row // BS, (start + column) // BS] == 0)
                def _():
                    out[row : row + BS, column : column + BS] = jnp.zeros((BS, BS), out.dtype)


def mask_tile(tile, flags, spans):
    count = len(spans)
    return kernel_call(
        functools.partial(mask_tile_kernel, spans),
        "mask_tile_%d" % len(spans),
        [VMEM((tile.shape[0], width), tile.dtype) for _, width in spans],
        [pinned(flags, HBM), pinned(tile, HBM)],
        [HBM, HBM],
        VMEM,
        [pltpu.SMEM(flags.shape, flags.dtype), pltpu.SemaphoreType.DMA, pltpu.SemaphoreType.DMA((count,))],
    )


def choose_kernel(on_even, on_odd, out):
    odd = lax.axis_index("col") % 2

    @pl.when(odd == 0)
    def _():
        out[...] = on_even[...]

    @pl.when(odd == 1)
    def _():
        out[...] = on_odd[...]


def choose(name, on_even, on_odd):
    return kernel_call(
        choose_kernel,
        "choose_" + name,
        VMEM(on_even.shape, on_even.dtype),
        [pinned(on_even), pinned(on_odd)],
        [VMEM, VMEM],
        VMEM,
    )


def stack_rows_kernel(offsets, all_flags, *refs):
    *shards, out, flags, flag_sem, sem = refs
    rows = shards[0].shape[0]
    me, count = lax.axis_index("row"), len(shards)
    flag_copy = pltpu.make_async_copy(all_flags, flags, flag_sem)
    flag_copy.start()
    copies = []
    for n, (shard, (distance, flip)) in enumerate(zip(shards, offsets)):
        place = lax.rem(me + distance, count)
        if flip:
            place = place + 1 - 2 * lax.rem(place, 2)
        start = pl.multiple_of(place * rows, rows)
        copies.append(pltpu.make_async_copy(shard, out.at[pl.ds(start, rows), :], sem.at[n]))
    for copy in copies:
        copy.start()
    flag_copy.wait()
    for copy in copies:
        copy.wait()

    @pl.loop(0, out.shape[0] // BS)
    def _(block_row):
        where = pl.ds(pl.multiple_of(block_row * BS, BS), BS)
        for column in range(out.shape[1] // BS):

            @pl.when(flags[block_row, column] == 0)
            def _():
                out[where, column * BS : (column + 1) * BS] = jnp.zeros((BS, BS), out.dtype)


def stack_rows(shards, offsets, flags):
    rows, depth = shards[0].shape
    count = len(shards)
    return kernel_call(
        functools.partial(stack_rows_kernel, offsets),
        "stack_rows",
        VMEM((rows * count, depth), shards[0].dtype),
        [pinned(flags, HBM), *shards],
        [HBM] + [ANY] * count,
        VMEM,
        [pltpu.SMEM(flags.shape, flags.dtype), pltpu.SemaphoreType.DMA, pltpu.SemaphoreType.DMA((count,))],
    )


def sums(left, tiles, places, partial, rows, store):
    depth = tiles[0].shape[0]
    odd = lax.axis_index("col") % 2
    first = 0
    for terms in places:
        columns = slice(first, first + tiles[terms[0][0]].shape[1])
        first = columns.stop
        total = None if partial is None else partial[rows, columns]
        for number, on_even, on_odd in terms:
            start = on_even * depth
            if on_even != on_odd:
                start = pl.multiple_of(start + odd * ((on_odd - on_even) * depth), depth)
            term = jnp.dot(left[rows, pl.ds(start, depth)], tiles[number][...], preferred_element_type=jnp.float32)
            total = term if total is None else total + term
        store(columns, total)


def chunks_of(left):
    chunk = min(2 * BS, left.shape[0])
    return chunk, left.shape[0] // chunk


def sum_kernel(plan, left, *refs):
    groups, rights = plan
    tiles, outs = refs[:rights], refs[rights:]
    chunk, count = chunks_of(left)

    @pl.loop(0, count)
    def _(index):
        rows = pl.ds(pl.multiple_of(index * chunk, chunk), chunk)
        for places, out in zip(groups, outs):

            def store(columns, total):
                out[rows, columns] = total.astype(out.dtype)

            sums(left, tiles, places, None, rows, store)


def last_kernel(plan, left, *refs):
    places, rights, ready_columns, column = plan
    tiles, partial = refs[:rights], refs[rights]
    ready, (out, result, sem, ready_sem) = refs[rights + 1 : -4], refs[-4:]
    chunk, count = chunks_of(left)
    copies = [
        pltpu.make_async_copy(block, out.at[:, start : start + block.shape[1]], ready_sem.at[n])
        for n, (block, start) in enumerate(zip(ready, ready_columns))
    ]
    for copy in copies:
        copy.start()

    def out_copy(index):
        rows = pl.ds(pl.multiple_of(index * chunk, chunk), chunk)
        return pltpu.make_async_copy(
            result.at[index], out.at[rows, column : column + result.shape[2]], sem.at[index]
        )

    @pl.loop(0, count)
    def _(index):
        rows = pl.ds(pl.multiple_of(index * chunk, chunk), chunk)

        def store(columns, total):
            result[index, :, columns] = total.astype(out.dtype)

        sums(left, tiles, places, partial, rows, store)
        out_copy(index).start()

    for copy in copies:
        copy.wait()

    @pl.loop(0, count)
    def _(index):
        out_copy(index).wait()


def number_terms(places):
    tiles = []
    for terms in places:
        for tile, _, _ in terms:
            if not any(tile is known for known in tiles):
                tiles.append(tile)
    numbered = tuple(
        tuple((next(n for n, known in enumerate(tiles) if known is tile), a, b) for tile, a, b in terms)
        for terms in places
    )
    return tiles, numbered


def add_products(name, left, groups, dtypes):
    tiles, numbered = number_terms([terms for places in groups for terms in places])
    rows = left.shape[0]
    numbered_groups, out_shapes = [], []
    for places, dtype in zip(groups, dtypes):
        numbered_groups.append(numbered[: len(places)])
        numbered = numbered[len(places) :]
        out_shapes.append(VMEM((rows, sum(terms[0][0].shape[1] for terms in places)), dtype))
    operands = [pinned(x) for x in (left, *tiles)]
    return kernel_call(
        functools.partial(sum_kernel, (tuple(numbered_groups), len(tiles))),
        "sum_" + name,
        out_shapes,
        operands,
        [VMEM] * len(operands),
        VMEM,
        flops=2 * rows * sum(tile.size for places in groups for terms in places for tile, _, _ in terms),
    )


def finish_product(left, places, column, width, partial, ready):
    tiles, numbered = number_terms(places)
    rows = left.shape[0]
    columns = sum(terms[0][0].shape[1] for terms in places)
    chunk, count = chunks_of(left)
    operands = [pinned(x) for x in (left, *tiles, partial, *[block for block, _ in ready])]
    plan = (numbered, len(tiles), tuple(start for _, start in ready), column)
    return kernel_call(
        functools.partial(last_kernel, plan),
        "sum_last",
        jax.ShapeDtypeStruct((rows, width), left.dtype),
        operands,
        [VMEM] * len(operands),
        HBM,
        [
            pltpu.VMEM((count, chunk, columns), left.dtype),
            pltpu.SemaphoreType.DMA((count,)),
            pltpu.SemaphoreType.DMA((len(ready),)),
        ],
        flops=2 * rows * sum(tile.size for terms in places for tile, _, _ in terms),
    )


def moved(block, axis, target):
    count = lax.axis_size(axis)
    return lax.ppermute(block, axis, [(i, target(i) % count) for i in range(count)])


def tied(value, *entries):
    value, *others = lax.optimization_barrier((value, *[entry[0] for entry in entries]))
    for entry, other in zip(entries, others):
        entry[0] = other
    return value


HELD = {
    "Sb": ["Db", "own_c"],
    "Zc": ["Sb"],
    "Q": ["Y12", "Ar", "own_c", "X", "own_b", "Ax"],
    "Ar": ["Z12", "Zb"],
    "last": ["Zc", "Af", "Db", "Ar", "Zb", "Z12", "Sc", "Q"],
    "Y12": ["Sb"],
    "early": ["Af"],
    "W12": ["Z12"],
}


def shards(a_window, b_tiles, mask_a, mask_b):
    width = b_tiles.shape[1]
    count = lax.axis_size("row")
    got = {}

    def held(name, value):
        names = HELD.get(name, [])
        return tied(value, *[got[known] for known in names]) if names else value

    def send(name, block, axis, target, key=None):
        with jax.named_scope("send_" + name):
            got[key or name] = [moved(held(name, block), axis, target)]
        return got[key or name][0]

    def by_two(name, block):
        return send(name, block, "col", lambda i: i - 2)

    def across(name, block):
        return send(name, block, "col", lambda i: i ^ 1)

    def value(name):
        return got[name][0]

    piece = width // PIECES
    (own_b,) = mask_tile(b_tiles, mask_b, ((0, piece),))
    got["own_b"] = [own_b]
    by_two("Zb", own_b)
    across("Db", own_b)
    own_c, own_12 = mask_tile(tied(b_tiles, [own_b]), mask_b, ((piece, piece), (2 * piece, 2 * piece)))
    got["own_c"] = [own_c]
    by_two("Z12", own_12)
    mine = a_window

    lefts, offsets = [mine], [(0, False)]
    for distance in range(2, count, 2):
        send("Ax", mine, "row", lambda i: i - distance, f"Ax{distance}")
        got["Ax"] = got[f"Ax{distance}"]
        offsets.append((distance, False))
    across("Sb", value("Zb"))
    send("Af", mine, "row", lambda i: i ^ 1)
    by_two("Zc", own_c)
    across("Y12", choose("Y12", value("Z12"), own_12))
    by_two("X", choose("X", value("Zc"), value("Sb")))
    across("Sc", value("Zc"))
    for distance in range(2, count, 2):
        send("Ar", value(f"Ax{distance}"), "row", lambda i: i ^ 1, f"Ar{distance}")
        got["Ar"] = got[f"Ar{distance}"]
    lefts += [value(f"Ax{distance}") for distance in range(2, count, 2)]
    lefts += [value("Af")] + [value(f"Ar{distance}") for distance in range(2, count, 2)]
    offsets += [(distance, True) for distance, _ in offsets]
    left = stack_rows(lefts, tuple(offsets), mask_a)
    column_b = [(own_b, 0, 0), (value("Zb"), 2, 2), (value("Sb"), 3, 1), (choose("b", value("Db"), value("X")), 1, 3)]
    by_two("W12", value("Y12"))
    across("Q", choose("Q", value("X"), own_c))

    column_12 = [(own_12, 0, 0), (value("Y12"), 1, 1), (value("Z12"), 2, 2)]
    column_c = [(own_c, 0, 0), (value("Zc"), 2, 2), (value("Sc"), 3, 1)]
    first, partial = add_products(
        "early", held("early", left), [[column_b], [column_c, column_12]], [left.dtype, jnp.float32]
    )
    return finish_product(
        held("last", left),
        [[(value("Q"), 1, 3)], [(value("W12"), 3, 3)]],
        piece,
        width,
        partial,
        [(first, 0)],
    )


def solution(mesh):
    return jax.shard_map(
        shards,
        mesh=mesh,
        in_specs=(P(("col", "row"), None), P("col", "row"), P("col", None), P("col", "row")),
        out_specs=P("col", "row"),
        check_vma=False,
    )
```
